32 devices in a mesh: gx: 8 (over y, x, core), gy: 4 (over z).
Axes of the slice: x: 2, y: 2, z: 4, core: 2. Of those that a mesh axis runs over, the one named last changes fastest.
Arguments:
- estimate: float32 [128, 64, 128], P('gx', 'gy'), may hold values from -6 to 6
- measured: float32 [128, 64, 128], P('gx', 'gy'), may hold values from -6 to 6
- weights: float32 [4, 128, 64, 128], P(None, 'gx', 'gy'), may hold values from 0.3 to 3
- kernels: float32 [4, 3, 15], replicated, may hold values from -0.6 to 0.6
- step_size: float32 [1], replicated, may hold values from 0.1 to 0.25
- penalty: float32 [1], replicated, may hold values from 0.2 to 1
Outputs:
- current: float32 [128, 64, 128], P('gx', 'gy')
- extrapolated: float32 [128, 64, 128], P('gx', 'gy')
The draws below stay inside these ranges and needn't reach their ends.
All inputs are finite; a program needn't handle non-finite values.
Results may differ from the reference program's by a relative error of at most 0.0003.
Values sent between devices are 32-bit elements; how exact they have to be, the bound alone decides.
A program may use at most 64 MiB of HBM per device.

```python
import math
import jax
import jax.numpy as jnp
from jax import lax

NZ = 128
TAPS = 15
RANKS = 4
ITERS = 2
NX = 128
NY = 64


def level_of(stream_key, shape, cuts, smallest, top_value):
    def one(dim, blocks):
        draws = jax.random.uniform(jax.random.fold_in(jax.random.fold_in(stream_key, 6), dim), (blocks,), jnp.float32, smallest / len(cuts), top_value / len(cuts))
        return jnp.repeat(jnp.exp(draws), shape[dim] // blocks).reshape((-1,) + (1,) * (len(shape) - dim - 1))

    loudness = one(*cuts[0])
    for cut in cuts[1:]:
        loudness = loudness * one(*cut)
    return loudness


def bell_draw(stream_key, shape, deviation, bound, shards=(), kind=jnp.bfloat16):
    loudness = level_of(stream_key, shape, shards, -0.22, 0.18) if shards else 1.0
    entries = jax.random.normal(stream_key, shape, jnp.float32) * deviation * loudness
    return jnp.minimum(jnp.maximum(entries, -bound), bound).astype(kind)


def setup_inputs(seed: int = 0) -> dict:
    streams_of = jax.random.split(jax.random.key(seed), 7)
    estimate = bell_draw(streams_of[0], (NX, NY, NZ), 1.0, 6.0, ((0, 8), (1, 4)), jnp.float32)
    measured = bell_draw(streams_of[1], (NX, NY, NZ), 1.0, 6.0, ((0, 8), (1, 4)), jnp.float32)
    weights = jnp.clip(jnp.exp(math.log(3.0) - 2.3025851 * jax.random.uniform(streams_of[2], (RANKS, NX, NY, NZ), jnp.float32) ** level_of(streams_of[2], (RANKS, NX, NY, NZ), ((1, 8), (2, 4)), -0.2, 0.2)), 0.3, 3.0)
    kernels = bell_draw(streams_of[3], (RANKS, 3, TAPS), 0.15, 0.6, (), jnp.float32)
    step_size = jnp.clip(jax.random.uniform(streams_of[4], (1,), jnp.float32, 0.1, 0.25), 0.1, 0.25)
    penalty = jnp.clip(jax.random.uniform(streams_of[5], (1,), jnp.float32, 0.2, 1.0), 0.2, 1.0)
    return {"estimate": estimate, "measured": measured, "weights": weights, "kernels": kernels, "step_size": step_size, "penalty": penalty}


def correlate(volume, kernel, along):
    extent = volume.shape[along]
    margin = kernel.shape[0] // 2
    widths = [(0, 0), (0, 0), (0, 0)]
    widths[along] = (margin, margin)
    padded = jnp.pad(volume, widths)
    summed = jnp.zeros_like(volume)
    for offset in range(kernel.shape[0]):
        summed = summed + kernel[offset] * lax.slice_in_dim(padded, offset, offset + extent, axis=along)
    return summed

def blur(volume, kernels, member, flip):
    for along in (2, 1, 0):
        kernel = kernels[member, along]
        if flip:
            kernel = kernel[::-1]
        volume = correlate(volume, kernel, along)
    return volume

def forward(volume, weights, kernels):
    summed = jnp.zeros_like(volume)
    for member in range(RANKS):
        summed = summed + weights[member] * blur(volume, kernels, member, False)
    return summed

def adjoint(volume, weights, kernels):
    summed = jnp.zeros_like(volume)
    for member in range(RANKS):
        summed = summed + blur(weights[member] * volume, kernels, member, True)
    return summed

def reference(estimate, measured, weights, kernels, step_size, penalty):
    step_scale = step_size[0]
    shrink = step_scale * penalty[0]
    current = estimate
    extrapolated = estimate
    momentum = 1.0
    for iteration in range(ITERS):
        residual = forward(extrapolated, weights, kernels) - measured
        gradient = adjoint(residual, weights, kernels)
        moved = extrapolated - step_scale * gradient
        updated = jnp.sign(moved) * jnp.maximum(jnp.abs(moved) - shrink, 0.0)
        following = (1.0 + math.sqrt(1.0 + 4.0 * momentum * momentum)) / 2.0
        extrapolated = updated + (momentum - 1.0) / following * (updated - current)
        current = updated
        momentum = following
    return (current, extrapolated)
```

```python
import functools
import math

import jax
import jax.numpy as jnp
from jax import lax
from jax.experimental import pallas as pl
from jax.experimental.pallas import tpu as pltpu
from jax.sharding import PartitionSpec as P

ITERS = 2
SUBLANES = 8
MESH = pl.DeviceIdType.MESH
SIDES = [(0, -1), (0, 1), (-1, 0), (1, 0), (-1, -1), (-1, 1), (1, -1), (1, 1)]
F32 = jnp.float32
BF16 = jnp.bfloat16


def log2(n):
    assert n & (n - 1) == 0
    return n.bit_length() - 1


def split(value):
    high = value.astype(BF16)
    low = (value - high.astype(F32)).astype(BF16)
    return high, low


def kernel(
    nx, ny, rows, cols, depth, taps, ranks,
    k_ref, step_ref, pen_ref, est_ref, meas_ref, w_ref,
    cur_ref, ext_ref,
    x_ref, m_ref, wv_ref, hz, hx, hc, gz, gx_, gc,
    a0, a1, b0, b1, sf, sa, zf, za, acc, v_ref,
    local_sem, send_sem, recv_sem,
):
    margin = taps // 2
    wide = -(-margin // SUBLANES) * SUBLANES
    tall = -(-margin // SUBLANES) * SUBLANES
    own = rows * cols
    gx = lax.axis_index("gx")
    gy = lax.axis_index("gy")

    def there(side):
        ok = None
        for at, by, count in ((gx, side[0], nx), (gy, side[1], ny)):
            if by == 0:
                continue
            one = (at + by >= 0) & (at + by < count)
            ok = one if ok is None else ok & one
        return ok

    def slot(bufs, lead, side):
        z, x, c = bufs
        n = SIDES.index(side)
        if n < 2:
            return z.at[lead, n]
        if n < 4:
            return x.at[lead, n - 2, pl.ds(0, margin)]
        return c.at[lead, n - 4, pl.ds(0, margin)]

    def edge(ref, side):
        dx, dy = side
        r = {0: (0, rows), -1: (0, margin), 1: (rows - margin, margin)}[dx]
        c = {0: (0, cols), -1: (0, wide), 1: (cols - wide, wide)}[dy]
        return ref.at[pl.ds(*r), pl.ds(*c)]

    halo = (hz, hx, hc)

    def transfer(phase, side, src):
        back = (-side[0], -side[1])
        return pltpu.make_async_remote_copy(
            src_ref=src,
            dst_ref=slot(halo, phase, back),
            send_sem=send_sem.at[phase, SIDES.index(side)],
            recv_sem=recv_sem.at[phase, SIDES.index(back)],
            device_id=(gx + side[0], gy + side[1]),
            device_id_type=MESH,
        )

    def source(phase, side):
        if phase % 2 == 1:
            return slot((gz, gx_, gc), phase // 2, side)
        return edge(est_ref if phase == 0 else x_ref, side)

    def send(phase, sides):
        for side in sides:
            @pl.when(there(side))
            def _():
                transfer(phase, side, source(phase, side)).start()

    def receive(phase, sides):
        for side in sides:
            back = (-side[0], -side[1])

            @pl.when(there(side))
            def _():
                transfer(phase, back, source(phase, back)).wait_recv()

    copies = [
        pltpu.make_async_copy(est_ref, x_ref, local_sem.at[0]),
        pltpu.make_async_copy(meas_ref, m_ref, local_sem.at[1]),
        pltpu.make_async_copy(w_ref, wv_ref, local_sem.at[2]),
    ]
    for copy in copies:
        copy.start()

    barrier = pltpu.get_barrier_semaphore()
    near = 0
    for side in SIDES:
        @pl.when(there(side))
        def _():
            pl.semaphore_signal(
                barrier, inc=1, device_id=(gx + side[0], gy + side[1]), device_id_type=MESH
            )
        near = near + there(side).astype(jnp.int32)
    pl.semaphore_wait(barrier, near)
    order = SIDES[4:] + SIDES[:4]
    send(0, order)

    for phase in range(2 * ITERS):
        for n in range(2):
            hx[phase, n, margin:] = jnp.zeros((tall - margin, cols, depth), F32)
        for n in range(4):
            hc[phase, n, margin:] = jnp.zeros((tall - margin, wide, depth), F32)
        for side in SIDES:
            @pl.when(jnp.logical_not(there(side)))
            def _():
                ref = slot(halo, phase, side)
                ref[...] = jnp.zeros(ref.shape, F32)

    tile = own

    def places(t, shape, dim):
        at = lax.broadcasted_iota(jnp.int32, shape, dim)
        if t == 0:
            return at >> log2(cols), at & (cols - 1)
        if t == 1:
            half = rows * wide
            p = (at & (half - 1)) >> log2(wide)
            q = at & (wide - 1)
            return p, jnp.where(at >= half, q + cols, q - wide)
        if t == 2:
            half = tall * cols
            p = (at & (half - 1)) >> log2(cols)
            q = at & (cols - 1)
            return jnp.where(at >= half, p + rows, p - margin), q
        part = tall * wide
        n = at >> log2(part)
        p = (at & (part - 1)) >> log2(wide)
        q = at & (wide - 1)
        return (
            jnp.where(n >= 2, p + rows, p - margin),
            jnp.where((n & 1) == 1, q + cols, q - wide),
        )

    def banded(gap, m, axis):
        out = jnp.zeros(gap.shape, F32)
        for t in range(taps):
            out = jnp.where(gap == t, k_ref[m, axis, t], out)
        return out

    for t in range(4):
        shape = (rows, tile)
        p, q = places(t, shape, 1)
        gap_p = p - lax.broadcasted_iota(jnp.int32, shape, 0) + margin
        gap_q = q - lax.broadcasted_iota(jnp.int32, (cols, tile), 0) + margin

        def table(m, _):
            a0[m, :, t * tile:(t + 1) * tile] = banded(gap_p, m, 0)
            a1[m, :, t * tile:(t + 1) * tile] = banded(gap_q, m, 1)
            return 0

        lax.fori_loop(0, ranks, table, 0)

    def fill_forward(u, _):
        m, i = u >> log2(rows), u & (rows - 1)
        at = pl.ds(pl.multiple_of(u * cols, cols), cols)
        for t in range(4):
            span = slice(t * tile, (t + 1) * tile)
            high, low = split(a0[m, pl.ds(i, 1), span] * a1[m, :, span])
            sf[at, 2 * t * tile:(2 * t + 1) * tile] = high
            sf[at, (2 * t + 1) * tile:(2 * t + 2) * tile] = low
        return 0

    lax.fori_loop(0, ranks * rows, fill_forward, 0)

    gap_z = (
        lax.broadcasted_iota(jnp.int32, (depth, depth), 0)
        - lax.broadcasted_iota(jnp.int32, (depth, depth), 1)
        + margin
    )

    def optical(m, _):
        for ref, gap in ((zf, gap_z), (za, 2 * margin - gap_z)):
            high, low = split(banded(gap, m, 2))
            ref[m, :depth, :depth] = high
            ref[m, :depth, depth:] = low
            ref[m, depth:, :depth] = high
            ref[m, depth:, depth:] = jnp.zeros((depth, depth), BF16)
        return 0

    lax.fori_loop(0, ranks, optical, 0)

    lane_i, lane_j = places(0, (b0.shape[1], tile), 1)
    gap_i = lax.broadcasted_iota(jnp.int32, lane_i.shape, 0) - lane_i
    gap_j = lax.broadcasted_iota(jnp.int32, lane_j.shape, 0) - wide - lane_j + margin

    def table_back(m, _):
        b0[m] = banded(gap_i, m, 0)
        b1[m] = banded(gap_j, m, 1)
        return 0

    lax.fori_loop(0, ranks, table_back, 0)

    def put(start, first, qs):
        at = pl.ds(pl.multiple_of(start, 2 * SUBLANES), 2 * SUBLANES)
        for m in range(ranks):
            cells = [b0[m, pl.ds(f, 1), :] * b1[m, qs, :] for f in first]
            cells = cells[0] if len(cells) == 1 else jnp.concatenate(cells, 0)
            high, low = split(cells)
            sa[at, 2 * m * tile:(2 * m + 1) * tile] = high
            sa[at, (2 * m + 1) * tile:(2 * m + 2) * tile] = low

    middle = slice(wide, wide + cols)
    flanks = (slice(0, wide), slice(wide + cols, wide + cols + wide))

    def fill_own(p, _):
        put(p * cols, (p + margin,), middle)
        return 0

    def fill_z(u, _):
        for n in range(2):
            put(tile + n * rows * wide + u * 2 * wide, (2 * u + margin, 2 * u + 1 + margin), flanks[n])
        return 0

    def fill_x(u, _):
        for n in range(2):
            put(2 * tile + n * tall * cols + u * cols, (u + n * (rows + margin),), middle)
        return 0

    def fill_c(u, _):
        for n in range(4):
            first = 2 * u + (n // 2) * (rows + margin)
            put(3 * tile + n * tall * wide + u * 2 * wide, (first, first + 1), flanks[n % 2])
        return 0

    lax.fori_loop(0, rows, fill_own, 0)
    lax.fori_loop(0, rows // 2, fill_z, 0)
    lax.fori_loop(0, tall, fill_x, 0)
    lax.fori_loop(0, tall // 2, fill_c, 0)

    for copy in copies:
        copy.wait()

    step = step_ref[0]
    shrink = step * pen_ref[0]
    groups = [None, SIDES[0:2], SIDES[2:4], SIDES[4:8]]

    def doubled(cells):
        return jnp.concatenate([jnp.concatenate(split(cells), 1)] * 2, 0)

    def both(pair):
        return pair[:, :depth] + pair[:, depth:]

    momentum = 1.0
    for iteration in range(ITERS):
        phase = 2 * iteration
        for t in range(4):
            if t == 0:
                cells = x_ref[...]
            else:
                receive(phase, groups[t])
                cells = halo[t - 1][phase]
            right = doubled(cells.reshape(tile, depth))
            for m in range(ranks):
                at = slice(m * own, (m + 1) * own)
                part = jnp.dot(
                    sf[at, 2 * t * tile:(2 * t + 2) * tile], right, preferred_element_type=F32
                )
                acc[at] = part if t == 0 else acc[at] + part
        residual = -m_ref[...].reshape(own, depth)
        for m in range(ranks):
            at = slice(m * own, (m + 1) * own)
            mixed = jnp.concatenate(split(both(acc[at])), 1)
            blurred = both(jnp.dot(mixed, zf[m], preferred_element_type=F32))
            residual = residual + wv_ref[m].reshape(own, depth) * blurred
        for m in range(ranks):
            mixed = jnp.concatenate(split(wv_ref[m].reshape(own, depth) * residual), 1)
            back = both(jnp.dot(mixed, za[m], preferred_element_type=F32))
            v_ref[2 * m * tile:(2 * m + 2) * tile] = doubled(back)

        def spread(t):
            return both(
                jnp.dot(sa[t * tile:(t + 1) * tile], v_ref[...], preferred_element_type=F32)
            )

        phase = phase + 1
        outgoing = (gz, gx_, gc)
        for t in (3, 1, 2):
            ref = outgoing[t - 1]
            ref[iteration] = spread(t).reshape(ref.shape[1:])
            send(phase, groups[t])
        acc[:own, :depth] = spread(0)
        grad = acc.at[:own, :depth]
        receive(phase, SIDES)
        total = grad[...].reshape(rows, cols, depth)
        inner = jnp.concatenate(
            [hz[phase, 0], hz[phase, 1]], 1
        ) if cols == 2 * wide else None
        total = total + inner
        lower = jnp.concatenate([hc[phase, 0], hc[phase, 1]], 1) + hx[phase, 0]
        upper = jnp.concatenate([hc[phase, 2], hc[phase, 3]], 1) + hx[phase, 1]
        lower = lower[:margin]
        upper = upper[:margin]
        gap = jnp.zeros((rows - margin, cols, depth), F32)
        total = total + jnp.concatenate([lower, gap], 0) + jnp.concatenate([gap, upper], 0)
        extrapolated = x_ref[...]
        current = extrapolated if iteration == 0 else cur_ref[...]
        moved = extrapolated - step * total
        updated = jnp.where(
            moved > shrink, moved - shrink, jnp.where(moved < -shrink, moved + shrink, 0.0)
        )
        following = (1.0 + math.sqrt(1.0 + 4.0 * momentum * momentum)) / 2.0
        extrapolated = updated + (momentum - 1.0) / following * (updated - current)
        cur_ref[...] = updated
        momentum = following
        if iteration + 1 < ITERS:
            x_ref[...] = extrapolated
            send(phase + 1, order)
        else:
            ext_ref[...] = extrapolated

    for phase in range(2 * ITERS):
        for side in SIDES:
            @pl.when(there(side))
            def _():
                transfer(phase, side, source(phase, side)).wait_send()


def on_device(nx, ny, estimate, measured, weights, kernels, step_size, penalty):
    rows, cols, depth = estimate.shape
    ranks, _, taps = kernels.shape
    margin = taps // 2
    wide = -(-margin // SUBLANES) * SUBLANES
    tall = wide
    own = rows * cols
    assert cols == 2 * wide and rows == 2 * tall and ITERS >= 1
    phases = 2 * ITERS
    smem = pl.BlockSpec(memory_space=pltpu.SMEM)
    hbm = pl.BlockSpec(memory_space=pl.ANY)
    vmem = pl.BlockSpec(memory_space=pltpu.VMEM)

    def pieces(lead):
        return [
            pltpu.VMEM((lead, 2, rows, wide, depth), F32),
            pltpu.VMEM((lead, 2, tall, cols, depth), F32),
            pltpu.VMEM((lead, 4, tall, wide, depth), F32),
        ]

    out = jax.ShapeDtypeStruct(estimate.shape, F32)
    return pl.pallas_call(
        functools.partial(kernel, nx, ny, rows, cols, depth, taps, ranks),
        out_shape=(out, out),
        in_specs=[smem, smem, smem, hbm, hbm, hbm],
        out_specs=(vmem, vmem),
        scratch_shapes=[
            pltpu.VMEM(estimate.shape, F32),
            pltpu.VMEM(measured.shape, F32),
            pltpu.VMEM(weights.shape, F32),
            *pieces(phases),
            *pieces(ITERS),
            pltpu.VMEM((ranks, rows, 4 * own), F32),
            pltpu.VMEM((ranks, cols, 4 * own), F32),
            pltpu.VMEM((ranks, rows + 2 * tall, own), F32),
            pltpu.VMEM((ranks, cols + 2 * wide, own), F32),
            pltpu.VMEM((ranks * own, 8 * own), BF16),
            pltpu.VMEM((4 * own, 2 * ranks * own), BF16),
            pltpu.VMEM((ranks, 2 * depth, 2 * depth), BF16),
            pltpu.VMEM((ranks, 2 * depth, 2 * depth), BF16),
            pltpu.VMEM((ranks * own, 2 * depth), F32),
            pltpu.VMEM((2 * ranks * own, 2 * depth), BF16),
            pltpu.SemaphoreType.DMA((3,)),
            pltpu.SemaphoreType.DMA((phases, len(SIDES))),
            pltpu.SemaphoreType.DMA((phases, len(SIDES))),
        ],
        compiler_params=pltpu.CompilerParams(collective_id=0, has_side_effects=True),
        name="fista",
    )(kernels, step_size, penalty, estimate, measured, weights)


def solution(mesh):
    return jax.shard_map(
        functools.partial(on_device, mesh.shape["gx"], mesh.shape["gy"]),
        mesh=mesh,
        in_specs=(
            P("gx", "gy", None),
            P("gx", "gy", None),
            P(None, "gx", "gy", None),
            P(),
            P(),
            P(),
        ),
        out_specs=(P("gx", "gy", None), P("gx", "gy", None)),
        check_vma=False,
    )
```

```python
import functools
import math

import jax
import jax.numpy as jnp
from jax import lax
from jax.experimental import pallas as pl
from jax.experimental.pallas import tpu as pltpu
from jax.sharding import PartitionSpec as P

ITERS = 2
SUBLANES = 8
MESH = pl.DeviceIdType.MESH
SIDES = [(0, -1), (0, 1), (-1, 0), (1, 0), (-1, -1), (-1, 1), (1, -1), (1, 1)]
F32 = jnp.float32
BF16 = jnp.bfloat16


def log2(n):
    assert n & (n - 1) == 0
    return n.bit_length() - 1


def weight_of(iteration):
    momentum = 1.0
    for _ in range(iteration + 1):
        before, momentum = momentum, (1.0 + math.sqrt(1.0 + 4.0 * momentum * momentum)) / 2.0
    return (before - 1.0) / momentum


def split(value):
    high = value.astype(BF16)
    low = (value - high.astype(F32)).astype(BF16)
    return high, low


def kernel(
    nx, ny, rows, cols, depth, taps, ranks,
    k_ref, step_ref, pen_ref, est_ref, meas_ref, w_ref,
    delta_ref, cur_ref,
    x_ref, m_ref, wv_ref, hz, hx, hc, gz, gx_, gc,
    a0, a1, b0, b1, sf, sa, zf, za, acc, v_ref,
    local_sem, send_sem, recv_sem,
):
    margin = taps // 2
    wide = -(-margin // SUBLANES) * SUBLANES
    tall = -(-margin // SUBLANES) * SUBLANES
    own = rows * cols
    gx = lax.axis_index("gx")
    gy = lax.axis_index("gy")

    def there(side):
        ok = None
        for at, by, count in ((gx, side[0], nx), (gy, side[1], ny)):
            if by == 0:
                continue
            one = (at + by >= 0) & (at + by < count)
            ok = one if ok is None else ok & one
        return ok

    def slot(bufs, lead, side, turned=False):
        z, x, c = bufs
        n = SIDES.index(side)
        q = pl.ds(wide - margin if (side[1] < 0) != turned else 0, margin)
        if n < 2:
            return z.at[lead, n, :, q]
        if n < 4:
            return x.at[lead, n - 2, pl.ds(0, margin)]
        return c.at[lead, n - 4, pl.ds(0, margin), q]

    def edge(ref, side):
        dx, dy = side
        r = {0: (0, rows), -1: (0, margin), 1: (rows - margin, margin)}[dx]
        c = {0: (0, cols), -1: (0, margin), 1: (cols - margin, margin)}[dy]
        return ref.at[pl.ds(*r), pl.ds(*c)]

    halo = (hz, hx, hc)

    def transfer(phase, side, src):
        back = (-side[0], -side[1])
        return pltpu.make_async_remote_copy(
            src_ref=src,
            dst_ref=slot(halo, phase, back, phase % 2 == 1),
            send_sem=send_sem.at[phase, SIDES.index(side)],
            recv_sem=recv_sem.at[phase, SIDES.index(back)],
            device_id=(gx + side[0], gy + side[1]),
            device_id_type=MESH,
        )

    def source(phase, side):
        if phase % 2 == 1:
            return slot((gz, gx_, gc), phase // 2, side)
        return edge(est_ref if phase == 0 else x_ref, side)

    def send(phase, sides):
        for side in sides:
            @pl.when(there(side))
            def _():
                transfer(phase, side, source(phase, side)).start()

    def receive(phase, sides):
        for side in sides:
            back = (-side[0], -side[1])

            @pl.when(there(side))
            def _():
                transfer(phase, back, source(phase, back)).wait_recv()

    copies = [
        pltpu.make_async_copy(est_ref, x_ref, local_sem.at[0]),
        pltpu.make_async_copy(meas_ref, m_ref, local_sem.at[1]),
        pltpu.make_async_copy(w_ref, wv_ref, local_sem.at[2]),
    ]
    for copy in copies:
        copy.start()

    barrier = pltpu.get_barrier_semaphore()
    near = 0
    for side in SIDES:
        @pl.when(there(side))
        def _():
            pl.semaphore_signal(
                barrier, inc=1, device_id=(gx + side[0], gy + side[1]), device_id_type=MESH
            )
        near = near + there(side).astype(jnp.int32)
    pl.semaphore_wait(barrier, near)
    order = SIDES[4:] + SIDES[:4]
    send(0, order)

    spare = (slice(0, wide - margin), slice(margin, wide))
    for phase in range(2 * ITERS):
        for n in range(2):
            hx[phase, n, margin:] = jnp.zeros((tall - margin, cols, depth), F32)
        for n in range(2):
            hz[phase, n, :, spare[(n + phase) % 2]] = jnp.zeros((rows, wide - margin, depth), F32)
        for n in range(4):
            hc[phase, n, :, spare[(n + phase) % 2]] = jnp.zeros((tall, wide - margin, depth), F32)
            hc[phase, n, margin:] = jnp.zeros((tall - margin, wide, depth), F32)
        for side in SIDES:
            @pl.when(jnp.logical_not(there(side)))
            def _():
                ref = slot(halo, phase, side, phase % 2 == 1)
                ref[...] = jnp.zeros(ref.shape, F32)

    tile = own

    def places(t, shape, dim):
        at = lax.broadcasted_iota(jnp.int32, shape, dim)
        if t == 0:
            return at >> log2(cols), at & (cols - 1)
        if t == 1:
            half = rows * wide
            p = (at & (half - 1)) >> log2(wide)
            q = at & (wide - 1)
            return p, jnp.where(at >= half, q + cols, q - wide)
        if t == 2:
            half = tall * cols
            p = (at & (half - 1)) >> log2(cols)
            q = at & (cols - 1)
            return jnp.where(at >= half, p + rows, p - margin), q
        part = tall * wide
        n = at >> log2(part)
        p = (at & (part - 1)) >> log2(wide)
        q = at & (wide - 1)
        return (
            jnp.where(n >= 2, p + rows, p - margin),
            jnp.where((n & 1) == 1, q + cols, q - wide),
        )

    def banded(gap, m, axis):
        out = jnp.zeros(gap.shape, F32)
        for t in range(taps):
            out = jnp.where(gap == t, k_ref[axis, m, t], out)
        return out

    for t in range(4):
        shape = (rows, tile)
        p, q = places(t, shape, 1)
        gap_p = p - lax.broadcasted_iota(jnp.int32, shape, 0) + margin
        gap_q = q - lax.broadcasted_iota(jnp.int32, (cols, tile), 0) + margin

        def table(m, _):
            a0[m, :, t * tile:(t + 1) * tile] = banded(gap_p, m, 0)
            a1[m, :, t * tile:(t + 1) * tile] = banded(gap_q, m, 1)
            return 0

        lax.fori_loop(0, ranks, table, 0)

    def fill_forward(u, _):
        m, i = u >> log2(rows), u & (rows - 1)
        at = pl.ds(pl.multiple_of(u * cols, cols), cols)
        for t in range(4):
            span = slice(t * tile, (t + 1) * tile)
            high, low = split(a0[m, pl.ds(i, 1), span] * a1[m, :, span])
            sf[at, 2 * t * tile:(2 * t + 1) * tile] = high
            sf[at, (2 * t + 1) * tile:(2 * t + 2) * tile] = low
        return 0

    lax.fori_loop(0, ranks * rows, fill_forward, 0)

    gap_z = (
        lax.broadcasted_iota(jnp.int32, (depth, depth), 0)
        - lax.broadcasted_iota(jnp.int32, (depth, depth), 1)
        + margin
    )

    def optical(m, _):
        for ref, gap in ((zf, gap_z), (za, 2 * margin - gap_z)):
            high, low = split(banded(gap, m, 2))
            ref[m, :depth, :depth] = high
            ref[m, :depth, depth:] = low
            ref[m, depth:, :depth] = high
            ref[m, depth:, depth:] = jnp.zeros((depth, depth), BF16)
        return 0

    lax.fori_loop(0, ranks, optical, 0)

    lane_i, lane_j = places(0, (b0.shape[1], tile), 1)
    gap_i = lax.broadcasted_iota(jnp.int32, lane_i.shape, 0) - lane_i
    gap_j = lax.broadcasted_iota(jnp.int32, lane_j.shape, 0) - wide - lane_j + margin

    def table_back(m, _):
        b0[m] = banded(gap_i, m, 0)
        b1[m] = banded(gap_j, m, 1)
        return 0

    lax.fori_loop(0, ranks, table_back, 0)

    def put(t, start, first, qs):
        at = [
            pl.ds(pl.multiple_of((2 * t + half) * tile + start, 2 * SUBLANES), 2 * SUBLANES)
            for half in range(2)
        ]
        for m in range(ranks):
            cells = [b0[m, pl.ds(f, 1), :] * b1[m, qs, :] for f in first]
            cells = cells[0] if len(cells) == 1 else jnp.concatenate(cells, 0)
            high, low = split(cells)
            sa[at[0], m * own:(m + 1) * own] = high
            sa[at[1], m * own:(m + 1) * own] = low

    middle = slice(wide, wide + cols)
    flanks = (slice(0, wide), slice(wide + cols, wide + cols + wide))

    def fill_own(p, _):
        put(0, p * cols, (p + margin,), middle)
        return 0

    def fill_z(u, _):
        for n in range(2):
            put(1, n * rows * wide + u * 2 * wide, (2 * u + margin, 2 * u + 1 + margin), flanks[n])
        return 0

    def fill_x(u, _):
        for n in range(2):
            put(2, n * tall * cols + u * cols, (u + n * (rows + margin),), middle)
        return 0

    def fill_c(u, _):
        for n in range(4):
            first = 2 * u + (n // 2) * (rows + margin)
            put(3, n * tall * wide + u * 2 * wide, (first, first + 1), flanks[n % 2])
        return 0

    lax.fori_loop(0, rows, fill_own, 0)
    lax.fori_loop(0, rows // 2, fill_z, 0)
    lax.fori_loop(0, tall, fill_x, 0)
    lax.fori_loop(0, tall // 2, fill_c, 0)

    for copy in copies:
        copy.wait()

    step = step_ref[0]
    shrink = step * pen_ref[0]
    groups = [None, SIDES[0:2], SIDES[2:4], SIDES[4:8]]

    def doubled(cells):
        return jnp.concatenate([jnp.concatenate(split(cells), 1)] * 2, 0)

    def both(pair):
        return pair[:, :depth] + pair[:, depth:]

    for iteration in range(ITERS):
        phase = 2 * iteration
        for t in range(4):
            if t == 0:
                cells = x_ref[...]
            else:
                receive(phase, groups[t])
                cells = halo[t - 1][phase]
            right = doubled(cells.reshape(tile, depth))
            for m in range(ranks):
                at = slice(m * own, (m + 1) * own)
                part = jnp.dot(
                    sf[at, 2 * t * tile:(2 * t + 2) * tile], right, preferred_element_type=F32
                )
                acc[at] = part if t == 0 else acc[at] + part
        residual = -m_ref[...].reshape(own, depth)
        for m in range(ranks):
            at = slice(m * own, (m + 1) * own)
            mixed = jnp.concatenate(split(both(acc[at])), 1)
            blurred = both(jnp.dot(mixed, zf[m], preferred_element_type=F32))
            residual = residual + wv_ref[m].reshape(own, depth) * blurred
        for m in range(ranks):
            mixed = jnp.concatenate(split(wv_ref[m].reshape(own, depth) * residual), 1)
            back = both(jnp.dot(mixed, za[m], preferred_element_type=F32))
            v_ref[m * own:(m + 1) * own] = jnp.concatenate(split(back), 1)

        def spread(t):
            sums = jnp.dot(
                sa[2 * t * tile:(2 * t + 2) * tile], v_ref[...], preferred_element_type=F32
            )
            return both(sums[:tile] + sums[tile:])

        phase = phase + 1
        outgoing = (gz, gx_, gc)
        for t in (3, 1, 2):
            ref = outgoing[t - 1]
            ref[iteration] = spread(t).reshape(ref.shape[1:])
            send(phase, groups[t])
        acc[:own, :depth] = spread(0)
        grad = acc.at[:own, :depth]
        receive(phase, SIDES)
        total = grad[...].reshape(rows, cols, depth)
        inner = jnp.concatenate(
            [hz[phase, 0], hz[phase, 1]], 1
        ) if cols == 2 * wide else None
        total = total + inner
        lower = jnp.concatenate([hc[phase, 0], hc[phase, 1]], 1) + hx[phase, 0]
        upper = jnp.concatenate([hc[phase, 2], hc[phase, 3]], 1) + hx[phase, 1]
        lower = lower[:margin]
        upper = upper[:margin]
        gap = jnp.zeros((rows - margin, cols, depth), F32)
        total = total + jnp.concatenate([lower, gap], 0) + jnp.concatenate([gap, upper], 0)
        extrapolated = x_ref[...]
        current = extrapolated if iteration == 0 else cur_ref[...]
        moved = extrapolated - step * total
        updated = jnp.where(
            moved > shrink, moved - shrink, jnp.where(moved < -shrink, moved + shrink, 0.0)
        )
        if iteration + 1 == ITERS:
            delta_ref[...] = updated - current
            cur_ref[...] = current
            break
        x_ref[...] = updated + weight_of(iteration) * (updated - current)
        cur_ref[...] = updated
        send(phase + 1, order)

    for phase in range(2 * ITERS):
        for side in SIDES:
            @pl.when(there(side))
            def _():
                transfer(phase, side, source(phase, side)).wait_send()


def on_device(nx, ny, estimate, measured, weights, kernels, step_size, penalty):
    rows, cols, depth = estimate.shape
    ranks, _, taps = kernels.shape
    margin = taps // 2
    wide = -(-margin // SUBLANES) * SUBLANES
    tall = wide
    own = rows * cols
    assert cols == 2 * wide and rows == 2 * tall and ITERS >= 1
    phases = 2 * ITERS
    smem = pl.BlockSpec(memory_space=pltpu.SMEM)
    hbm = pl.BlockSpec(memory_space=pl.ANY)
    vmem = pl.BlockSpec(memory_space=pltpu.VMEM)

    def pieces(lead):
        return [
            pltpu.VMEM((lead, 2, rows, wide, depth), F32),
            pltpu.VMEM((lead, 2, tall, cols, depth), F32),
            pltpu.VMEM((lead, 4, tall, wide, depth), F32),
        ]

    out = jax.ShapeDtypeStruct(estimate.shape, F32)
    delta, current = pl.pallas_call(
        functools.partial(kernel, nx, ny, rows, cols, depth, taps, ranks),
        out_shape=(out, out),
        in_specs=[smem, smem, smem, hbm, hbm, hbm],
        out_specs=(vmem, vmem),
        scratch_shapes=[
            pltpu.VMEM(estimate.shape, F32),
            pltpu.VMEM(measured.shape, F32),
            pltpu.VMEM(weights.shape, F32),
            *pieces(phases),
            *pieces(ITERS),
            pltpu.VMEM((ranks, rows, 4 * own), F32),
            pltpu.VMEM((ranks, cols, 4 * own), F32),
            pltpu.VMEM((ranks, rows + 2 * tall, own), F32),
            pltpu.VMEM((ranks, cols + 2 * wide, own), F32),
            pltpu.VMEM((ranks * own, 8 * own), BF16),
            pltpu.VMEM((8 * own, ranks * own), BF16),
            pltpu.VMEM((ranks, 2 * depth, 2 * depth), BF16),
            pltpu.VMEM((ranks, 2 * depth, 2 * depth), BF16),
            pltpu.VMEM((ranks * own, 2 * depth), F32),
            pltpu.VMEM((ranks * own, 2 * depth), BF16),
            pltpu.SemaphoreType.DMA((3,)),
            pltpu.SemaphoreType.DMA((phases, len(SIDES))),
            pltpu.SemaphoreType.DMA((phases, len(SIDES))),
        ],
        compiler_params=pltpu.CompilerParams(collective_id=0, has_side_effects=True),
        name="fista",
    )(kernels.transpose(1, 0, 2), step_size, penalty, estimate, measured, weights)
    updated = current + delta
    return updated, updated + weight_of(ITERS - 1) * delta


def solution(mesh):
    return jax.shard_map(
        functools.partial(on_device, mesh.shape["gx"], mesh.shape["gy"]),
        mesh=mesh,
        in_specs=(
            P("gx", "gy", None),
            P("gx", "gy", None),
            P(None, "gx", "gy", None),
            P(),
            P(),
            P(),
        ),
        out_specs=(P("gx", "gy", None), P("gx", "gy", None)),
        check_vma=False,
    )
```

```python
import functools
import math

import jax
import jax.numpy as jnp
from jax import lax
from jax.experimental import pallas as pl
from jax.experimental.pallas import tpu as pltpu
from jax.sharding import PartitionSpec as P

ITERS = 2
SUBLANES = 8
GRANT = 24 << 20
MESH = pl.DeviceIdType.MESH
SIDES = [(0, -1), (0, 1), (-1, 0), (1, 0), (-1, -1), (-1, 1), (1, -1), (1, 1)]
F32 = jnp.float32
BF16 = jnp.bfloat16


def log2(n):
    assert n & (n - 1) == 0
    return n.bit_length() - 1


def weight_of(iteration):
    momentum = 1.0
    for _ in range(iteration + 1):
        before, momentum = momentum, (1.0 + math.sqrt(1.0 + 4.0 * momentum * momentum)) / 2.0
    return (before - 1.0) / momentum


def split(value):
    high = value.astype(BF16)
    low = (value - high.astype(F32)).astype(BF16)
    return high, low


def kernel(
    nx, ny, rows, cols, depth, taps, ranks,
    step_ref, pen_ref, taps_ref, est_ref, meas_ref, w_ref,
    delta_ref, cur_ref,
    k_ref, x_ref, m_ref, wv_ref, hz, hx, hc, gz, gx_, gc,
    a0, a1, b0, b1, sf, sa, zf, za, acc, v_ref,
    local_sem, send_sem, recv_sem,
):
    margin = taps // 2
    wide = -(-margin // SUBLANES) * SUBLANES
    tall = -(-margin // SUBLANES) * SUBLANES
    own = rows * cols
    gx = lax.axis_index("gx")
    gy = lax.axis_index("gy")

    def there(side):
        ok = None
        for at, by, count in ((gx, side[0], nx), (gy, side[1], ny)):
            if by == 0:
                continue
            one = (at + by >= 0) & (at + by < count)
            ok = one if ok is None else ok & one
        return ok

    def slot(bufs, lead, side, turned=False):
        z, x, c = bufs
        n = SIDES.index(side)
        q = pl.ds(wide - margin if (side[1] < 0) != turned else 0, margin)
        if n < 2:
            return z.at[lead, n, :, q]
        if n < 4:
            return x.at[lead, n - 2, pl.ds(0, margin)]
        return c.at[lead, n - 4, pl.ds(0, margin), q]

    def edge(ref, side):
        dx, dy = side
        r = {0: (0, rows), -1: (0, margin), 1: (rows - margin, margin)}[dx]
        c = {0: (0, cols), -1: (0, margin), 1: (cols - margin, margin)}[dy]
        return ref.at[pl.ds(*r), pl.ds(*c)]

    halo = (hz, hx, hc)

    def transfer(phase, side, src):
        back = (-side[0], -side[1])
        return pltpu.make_async_remote_copy(
            src_ref=src,
            dst_ref=slot(halo, phase, back, phase % 2 == 1),
            send_sem=send_sem.at[phase, SIDES.index(side)],
            recv_sem=recv_sem.at[phase, SIDES.index(back)],
            device_id=(gx + side[0], gy + side[1]),
            device_id_type=MESH,
        )

    def source(phase, side):
        if phase % 2 == 1:
            return slot((gz, gx_, gc), phase // 2, side)
        return edge(est_ref if phase == 0 else x_ref, side)

    def send(phase, sides):
        for side in sides:
            @pl.when(there(side))
            def _():
                transfer(phase, side, source(phase, side)).start()

    def receive(phase, sides):
        for side in sides:
            back = (-side[0], -side[1])

            @pl.when(there(side))
            def _():
                transfer(phase, back, source(phase, back)).wait_recv()

    copies = [
        pltpu.make_async_copy(est_ref, x_ref, local_sem.at[0]),
        pltpu.make_async_copy(meas_ref, m_ref, local_sem.at[1]),
        pltpu.make_async_copy(w_ref, wv_ref, local_sem.at[2]),
    ]
    copies.append(pltpu.make_async_copy(taps_ref, k_ref, local_sem.at[3]))
    barrier = pltpu.get_barrier_semaphore()
    near = 0
    for side in SIDES:
        @pl.when(there(side))
        def _():
            pl.semaphore_signal(
                barrier, inc=1, device_id=(gx + side[0], gy + side[1]), device_id_type=MESH
            )
        near = near + there(side).astype(jnp.int32)
    for copy in copies[::-1]:
        copy.start()
    pl.semaphore_wait(barrier, near)
    order = SIDES[4:] + SIDES[:4]
    send(0, order)

    spare = (slice(0, wide - margin), slice(margin, wide))
    for phase in range(2 * ITERS):
        for n in range(2):
            hx[phase, n, margin:] = jnp.zeros((tall - margin, cols, depth), F32)
        for n in range(2):
            hz[phase, n, :, spare[(n + phase) % 2]] = jnp.zeros((rows, wide - margin, depth), F32)
        for n in range(4):
            hc[phase, n, :, spare[(n + phase) % 2]] = jnp.zeros((tall, wide - margin, depth), F32)
            hc[phase, n, margin:] = jnp.zeros((tall - margin, wide, depth), F32)
        for side in SIDES:
            @pl.when(jnp.logical_not(there(side)))
            def _():
                ref = slot(halo, phase, side, phase % 2 == 1)
                ref[...] = jnp.zeros(ref.shape, F32)

    copies.pop().wait()

    tile = own

    def places(t, shape, dim):
        at = lax.broadcasted_iota(jnp.int32, shape, dim)
        if t == 0:
            return at >> log2(cols), at & (cols - 1)
        if t == 1:
            half = rows * wide
            p = (at & (half - 1)) >> log2(wide)
            q = at & (wide - 1)
            return p, jnp.where(at >= half, q + cols, q - wide)
        if t == 2:
            half = tall * cols
            p = (at & (half - 1)) >> log2(cols)
            q = at & (cols - 1)
            return jnp.where(at >= half, p + rows, p - margin), q
        part = tall * wide
        n = at >> log2(part)
        p = (at & (part - 1)) >> log2(wide)
        q = at & (wide - 1)
        return (
            jnp.where(n >= 2, p + rows, p - margin),
            jnp.where((n & 1) == 1, q + cols, q - wide),
        )

    def banded(gap, m, axis):
        out = jnp.zeros(gap.shape, F32)
        for t in range(taps):
            out = jnp.where(gap == t, k_ref[axis, m, t], out)
        return out

    for t in range(4):
        shape = (rows, tile)
        p, q = places(t, shape, 1)
        gap_p = p - lax.broadcasted_iota(jnp.int32, shape, 0) + margin
        gap_q = q - lax.broadcasted_iota(jnp.int32, (cols, tile), 0) + margin

        def table(m, _):
            a0[m, :, t * tile:(t + 1) * tile] = banded(gap_p, m, 0)
            a1[m, :, t * tile:(t + 1) * tile] = banded(gap_q, m, 1)
            return 0

        lax.fori_loop(0, ranks, table, 0)

    def fill_forward(u, _):
        m, i = u >> log2(rows), u & (rows - 1)
        at = pl.ds(pl.multiple_of(u * cols, cols), cols)
        for t in range(4):
            span = slice(t * tile, (t + 1) * tile)
            high, low = split(a0[m, pl.ds(i, 1), span] * a1[m, :, span])
            sf[at, 2 * t * tile:(2 * t + 1) * tile] = high
            sf[at, (2 * t + 1) * tile:(2 * t + 2) * tile] = low
        return 0

    lax.fori_loop(0, ranks * rows, fill_forward, 0)

    gap_z = (
        lax.broadcasted_iota(jnp.int32, (depth, depth), 0)
        - lax.broadcasted_iota(jnp.int32, (depth, depth), 1)
        + margin
    )

    def optical(m, _):
        for ref, gap in ((zf, gap_z), (za, 2 * margin - gap_z)):
            high, low = split(banded(gap, m, 2))
            ref[m, :depth, :depth] = high
            ref[m, :depth, depth:] = low
            ref[m, depth:, :depth] = high
            ref[m, depth:, depth:] = jnp.zeros((depth, depth), BF16)
        return 0

    lax.fori_loop(0, ranks, optical, 0)

    lane_i, lane_j = places(0, (b0.shape[1], tile), 1)
    gap_i = lax.broadcasted_iota(jnp.int32, lane_i.shape, 0) - lane_i
    gap_j = lax.broadcasted_iota(jnp.int32, lane_j.shape, 0) - wide - lane_j + margin

    def table_back(m, _):
        b0[m] = banded(gap_i, m, 0)
        b1[m] = banded(gap_j, m, 1)
        return 0

    lax.fori_loop(0, ranks, table_back, 0)

    def put(t, start, first, qs):
        at = [
            pl.ds(pl.multiple_of((2 * t + half) * tile + start, 2 * SUBLANES), 2 * SUBLANES)
            for half in range(2)
        ]
        for m in range(ranks):
            cells = [b0[m, pl.ds(f, 1), :] * b1[m, qs, :] for f in first]
            cells = cells[0] if len(cells) == 1 else jnp.concatenate(cells, 0)
            high, low = split(cells)
            sa[at[0], m * own:(m + 1) * own] = high
            sa[at[1], m * own:(m + 1) * own] = low

    middle = slice(wide, wide + cols)
    flanks = (slice(0, wide), slice(wide + cols, wide + cols + wide))

    def fill_own(p, _):
        put(0, p * cols, (p + margin,), middle)
        return 0

    def fill_z(u, _):
        for n in range(2):
            put(1, n * rows * wide + u * 2 * wide, (2 * u + margin, 2 * u + 1 + margin), flanks[n])
        return 0

    def fill_x(u, _):
        for n in range(2):
            put(2, n * tall * cols + u * cols, (u + n * (rows + margin),), middle)
        return 0

    def fill_c(u, _):
        for n in range(4):
            first = 2 * u + (n // 2) * (rows + margin)
            put(3, n * tall * wide + u * 2 * wide, (first, first + 1), flanks[n % 2])
        return 0

    lax.fori_loop(0, rows, fill_own, 0)
    lax.fori_loop(0, rows // 2, fill_z, 0)
    lax.fori_loop(0, tall, fill_x, 0)
    lax.fori_loop(0, tall // 2, fill_c, 0)

    for copy in copies:
        copy.wait()

    step = step_ref[0]
    shrink = step * pen_ref[0]
    groups = [None, SIDES[0:2], SIDES[2:4], SIDES[4:8]]

    def doubled(cells):
        return jnp.concatenate([jnp.concatenate(split(cells), 1)] * 2, 0)

    def both(pair):
        return pair[:, :depth] + pair[:, depth:]

    for iteration in range(ITERS):
        phase = 2 * iteration
        for t in range(4):
            if t == 0:
                cells = x_ref[...]
            else:
                receive(phase, groups[t])
                cells = halo[t - 1][phase]
            right = doubled(cells.reshape(tile, depth))
            for m in range(ranks):
                at = slice(m * own, (m + 1) * own)
                part = jnp.dot(
                    sf[at, 2 * t * tile:(2 * t + 2) * tile], right, preferred_element_type=F32
                )
                acc[at] = part if t == 0 else acc[at] + part
        residual = -m_ref[...].reshape(own, depth)
        for m in range(ranks):
            at = slice(m * own, (m + 1) * own)
            mixed = jnp.concatenate(split(both(acc[at])), 1)
            blurred = both(jnp.dot(mixed, zf[m], preferred_element_type=F32))
            residual = residual + wv_ref[m].reshape(own, depth) * blurred
        for m in range(ranks):
            mixed = jnp.concatenate(split(wv_ref[m].reshape(own, depth) * residual), 1)
            back = both(jnp.dot(mixed, za[m], preferred_element_type=F32))
            v_ref[m * own:(m + 1) * own] = jnp.concatenate(split(back), 1)

        def spread(t):
            sums = jnp.dot(
                sa[2 * t * tile:(2 * t + 2) * tile], v_ref[...], preferred_element_type=F32
            )
            return both(sums[:tile] + sums[tile:])

        phase = phase + 1
        outgoing = (gz, gx_, gc)
        for t in (3, 1, 2):
            ref = outgoing[t - 1]
            ref[iteration] = spread(t).reshape(ref.shape[1:])
            send(phase, groups[t])
        acc[:own, :depth] = spread(0)
        grad = acc.at[:own, :depth]
        receive(phase, SIDES)
        total = grad[...].reshape(rows, cols, depth)
        inner = jnp.concatenate(
            [hz[phase, 0], hz[phase, 1]], 1
        ) if cols == 2 * wide else None
        total = total + inner
        lower = jnp.concatenate([hc[phase, 0], hc[phase, 1]], 1) + hx[phase, 0]
        upper = jnp.concatenate([hc[phase, 2], hc[phase, 3]], 1) + hx[phase, 1]
        lower = lower[:margin]
        upper = upper[:margin]
        gap = jnp.zeros((rows - margin, cols, depth), F32)
        total = total + jnp.concatenate([lower, gap], 0) + jnp.concatenate([gap, upper], 0)
        extrapolated = x_ref[...]
        current = extrapolated if iteration == 0 else cur_ref[...]
        moved = extrapolated - step * total
        updated = jnp.where(
            moved > shrink, moved - shrink, jnp.where(moved < -shrink, moved + shrink, 0.0)
        )
        if iteration + 1 == ITERS:
            delta_ref[...] = updated - current
            cur_ref[...] = current
            break
        x_ref[...] = updated + weight_of(iteration) * (updated - current)
        cur_ref[...] = updated
        send(phase + 1, order)

    for phase in range(2 * ITERS):
        for side in SIDES:
            @pl.when(there(side))
            def _():
                transfer(phase, side, source(phase, side)).wait_send()


def on_device(nx, ny, estimate, measured, weights, kernels, step_size, penalty):
    rows, cols, depth = estimate.shape
    ranks, _, taps = kernels.shape
    margin = taps // 2
    wide = -(-margin // SUBLANES) * SUBLANES
    tall = wide
    own = rows * cols
    assert cols == 2 * wide and rows == 2 * tall and ITERS >= 1
    phases = 2 * ITERS
    smem = pl.BlockSpec(memory_space=pltpu.SMEM)
    hbm = pl.BlockSpec(memory_space=pltpu.HBM)
    vmem = pl.BlockSpec(memory_space=pltpu.VMEM)

    def pieces(lead):
        return [
            pltpu.VMEM((lead, 2, rows, wide, depth), F32),
            pltpu.VMEM((lead, 2, tall, cols, depth), F32),
            pltpu.VMEM((lead, 4, tall, wide, depth), F32),
        ]

    out = jax.ShapeDtypeStruct(estimate.shape, F32)
    delta, current = pl.pallas_call(
        functools.partial(kernel, nx, ny, rows, cols, depth, taps, ranks),
        out_shape=(out, out),
        in_specs=[smem, smem, hbm, hbm, hbm, hbm],
        out_specs=(vmem, vmem),
        scratch_shapes=[
            pltpu.SMEM((kernels.shape[1], ranks, taps), F32),
            pltpu.VMEM(estimate.shape, F32),
            pltpu.VMEM(measured.shape, F32),
            pltpu.VMEM(weights.shape, F32),
            *pieces(phases),
            *pieces(ITERS),
            pltpu.VMEM((ranks, rows, 4 * own), F32),
            pltpu.VMEM((ranks, cols, 4 * own), F32),
            pltpu.VMEM((ranks, rows + 2 * tall, own), F32),
            pltpu.VMEM((ranks, cols + 2 * wide, own), F32),
            pltpu.VMEM((ranks * own, 8 * own), BF16),
            pltpu.VMEM((8 * own, ranks * own), BF16),
            pltpu.VMEM((ranks, 2 * depth, 2 * depth), BF16),
            pltpu.VMEM((ranks, 2 * depth, 2 * depth), BF16),
            pltpu.VMEM((ranks * own, 2 * depth), F32),
            pltpu.VMEM((ranks * own, 2 * depth), BF16),
            pltpu.SemaphoreType.DMA((4,)),
            pltpu.SemaphoreType.DMA((phases, len(SIDES))),
            pltpu.SemaphoreType.DMA((phases, len(SIDES))),
        ],
        compiler_params=pltpu.CompilerParams(
            collective_id=0, has_side_effects=True, vmem_limit_bytes=GRANT
        ),
        name="fista",
    )(
        step_size,
        penalty,
        *(
            pltpu.with_memory_space_constraint(array, pltpu.HBM)
            for array in (kernels.transpose(1, 0, 2), estimate, measured, weights)
        ),
    )
    updated = current + delta
    return updated, updated + weight_of(ITERS - 1) * delta


def solution(mesh):
    return jax.shard_map(
        functools.partial(on_device, mesh.shape["gx"], mesh.shape["gy"]),
        mesh=mesh,
        in_specs=(
            P("gx", "gy", None),
            P("gx", "gy", None),
            P(None, "gx", "gy", None),
            P(),
            P(),
            P(),
        ),
        out_specs=(P("gx", "gy", None), P("gx", "gy", None)),
        check_vma=False,
    )
```

```python
import functools
import math

import jax
import jax.numpy as jnp
from jax import lax
from jax.experimental import pallas as pl
from jax.experimental.pallas import tpu as pltpu
from jax.sharding import PartitionSpec as P

ITERS = 2
SUBLANES = 8
GRANT = 24 << 20
MESH = pl.DeviceIdType.MESH
SIDES = [(0, -1), (0, 1), (-1, 0), (1, 0), (-1, -1), (-1, 1), (1, -1), (1, 1)]
F32 = jnp.float32
BF16 = jnp.bfloat16


def log2(n):
    assert n & (n - 1) == 0
    return n.bit_length() - 1


def weight_of(iteration):
    momentum = 1.0
    for _ in range(iteration + 1):
        before, momentum = momentum, (1.0 + math.sqrt(1.0 + 4.0 * momentum * momentum)) / 2.0
    return (before - 1.0) / momentum


def split(value):
    high = value.astype(BF16)
    low = (value - high.astype(F32)).astype(BF16)
    return high, low


def kernel(
    nx, ny, rows, cols, depth, taps, ranks,
    step_ref, pen_ref, taps_ref, est_ref, meas_ref, w_ref,
    delta_ref, cur_ref,
    k_ref, x_ref, m_ref, wv_ref, hz, hx, hc, gz, gx_, gc,
    a0, a1, b0, b1, sf, sa, zf, za, acc, v_ref,
    local_sem, send_sem, recv_sem,
):
    margin = taps // 2
    wide = -(-margin // SUBLANES) * SUBLANES
    tall = -(-margin // SUBLANES) * SUBLANES
    own = rows * cols
    gx = lax.axis_index("gx")
    gy = lax.axis_index("gy")

    def there(side):
        ok = None
        for at, by, count in ((gx, side[0], nx), (gy, side[1], ny)):
            if by == 0:
                continue
            one = (at + by >= 0) & (at + by < count)
            ok = one if ok is None else ok & one
        return ok

    def slot(bufs, lead, side, turned=False):
        z, x, c = bufs
        n = SIDES.index(side)
        q = pl.ds(wide - margin if (side[1] < 0) != turned else 0, margin)
        if n < 2:
            return z.at[lead, n, :, q]
        if n < 4:
            return x.at[lead, n - 2, pl.ds(0, margin)]
        return c.at[lead, n - 4, pl.ds(0, margin), q]

    def edge(ref, side):
        dx, dy = side
        r = {0: (0, rows), -1: (0, margin), 1: (rows - margin, margin)}[dx]
        c = {0: (0, cols), -1: (0, margin), 1: (cols - margin, margin)}[dy]
        return ref.at[pl.ds(*r), pl.ds(*c)]

    halo = (hz, hx, hc)

    def transfer(phase, side, src):
        back = (-side[0], -side[1])
        return pltpu.make_async_remote_copy(
            src_ref=src,
            dst_ref=slot(halo, phase, back, phase % 2 == 1),
            send_sem=send_sem.at[phase, SIDES.index(side)],
            recv_sem=recv_sem.at[phase, SIDES.index(back)],
            device_id=(gx + side[0], gy + side[1]),
            device_id_type=MESH,
        )

    def source(phase, side):
        if phase % 2 == 1:
            return slot((gz, gx_, gc), phase // 2, side)
        return edge(est_ref if phase == 0 else x_ref, side)

    def send(phase, sides):
        for side in sides:
            @pl.when(there(side))
            def _():
                transfer(phase, side, source(phase, side)).start()

    def receive(phase, sides):
        for side in sides:
            back = (-side[0], -side[1])

            @pl.when(there(side))
            def _():
                transfer(phase, back, source(phase, back)).wait_recv()

    copies = [
        pltpu.make_async_copy(est_ref, x_ref, local_sem.at[0]),
        pltpu.make_async_copy(meas_ref, m_ref, local_sem.at[1]),
        pltpu.make_async_copy(w_ref, wv_ref, local_sem.at[2]),
    ]
    copies.append(pltpu.make_async_copy(taps_ref, k_ref, local_sem.at[3]))
    barrier = pltpu.get_barrier_semaphore()
    near = 0
    for side in SIDES:
        @pl.when(there(side))
        def _():
            pl.semaphore_signal(
                barrier, inc=1, device_id=(gx + side[0], gy + side[1]), device_id_type=MESH
            )
        near = near + there(side).astype(jnp.int32)
    for copy in copies[::-1]:
        copy.start()
    pl.semaphore_wait(barrier, near)
    order = SIDES[:2] + SIDES[4:] + SIDES[2:4]
    send(0, order)

    spare = (slice(0, wide - margin), slice(margin, wide))
    for phase in range(2 * ITERS):
        for n in range(2):
            hx[phase, n, margin:] = jnp.zeros((tall - margin, cols, depth), F32)
        for n in range(2):
            hz[phase, n, :, spare[(n + phase) % 2]] = jnp.zeros((rows, wide - margin, depth), F32)
        for n in range(4):
            hc[phase, n, :, spare[(n + phase) % 2]] = jnp.zeros((tall, wide - margin, depth), F32)
            hc[phase, n, margin:] = jnp.zeros((tall - margin, wide, depth), F32)
        for side in SIDES:
            @pl.when(jnp.logical_not(there(side)))
            def _():
                ref = slot(halo, phase, side, phase % 2 == 1)
                ref[...] = jnp.zeros(ref.shape, F32)

    copies.pop().wait()

    tile = own

    def places(t, shape, dim):
        at = lax.broadcasted_iota(jnp.int32, shape, dim)
        if t == 0:
            return at >> log2(cols), at & (cols - 1)
        if t == 1:
            half = rows * wide
            p = (at & (half - 1)) >> log2(wide)
            q = at & (wide - 1)
            return p, jnp.where(at >= half, q + cols, q - wide)
        if t == 2:
            half = tall * cols
            p = (at & (half - 1)) >> log2(cols)
            q = at & (cols - 1)
            return jnp.where(at >= half, p + rows, p - margin), q
        part = tall * wide
        n = at >> log2(part)
        p = (at & (part - 1)) >> log2(wide)
        q = at & (wide - 1)
        return (
            jnp.where(n >= 2, p + rows, p - margin),
            jnp.where((n & 1) == 1, q + cols, q - wide),
        )

    def banded(gap, m, axis):
        out = jnp.zeros(gap.shape, F32)
        for t in range(taps):
            out = jnp.where(gap == t, k_ref[axis, m, t], out)
        return out

    for t in range(4):
        shape = (rows, tile)
        p, q = places(t, shape, 1)
        gap_p = p - lax.broadcasted_iota(jnp.int32, shape, 0) + margin
        gap_q = q - lax.broadcasted_iota(jnp.int32, (cols, tile), 0) + margin

        def table(m, _):
            a0[m, :, t * tile:(t + 1) * tile] = banded(gap_p, m, 0)
            a1[m, :, t * tile:(t + 1) * tile] = banded(gap_q, m, 1)
            return 0

        lax.fori_loop(0, ranks, table, 0)

    def fill_forward(u, _):
        m, i = u >> log2(rows), u & (rows - 1)
        at = pl.ds(pl.multiple_of(u * cols, cols), cols)
        for t in range(4):
            span = slice(t * tile, (t + 1) * tile)
            high, low = split(a0[m, pl.ds(i, 1), span] * a1[m, :, span])
            sf[at, 2 * t * tile:(2 * t + 1) * tile] = high
            sf[at, (2 * t + 1) * tile:(2 * t + 2) * tile] = low
        return 0

    lax.fori_loop(0, ranks * rows, fill_forward, 0)

    gap_z = (
        lax.broadcasted_iota(jnp.int32, (depth, depth), 0)
        - lax.broadcasted_iota(jnp.int32, (depth, depth), 1)
        + margin
    )

    def optical(m, _):
        for ref, gap in ((zf, gap_z), (za, 2 * margin - gap_z)):
            high, low = split(banded(gap, m, 2))
            ref[m, :depth, :depth] = high
            ref[m, :depth, depth:] = low
            ref[m, depth:, :depth] = high
            ref[m, depth:, depth:] = jnp.zeros((depth, depth), BF16)
        return 0

    lax.fori_loop(0, ranks, optical, 0)

    lane_i, lane_j = places(0, (b0.shape[1], tile), 1)
    gap_i = lax.broadcasted_iota(jnp.int32, lane_i.shape, 0) - lane_i
    gap_j = lax.broadcasted_iota(jnp.int32, lane_j.shape, 0) - wide - lane_j + margin

    def table_back(m, _):
        b0[m] = banded(gap_i, m, 0)
        b1[m] = banded(gap_j, m, 1)
        return 0

    lax.fori_loop(0, ranks, table_back, 0)

    def put(t, start, first, qs):
        at = [
            pl.ds(pl.multiple_of((2 * t + half) * tile + start, 2 * SUBLANES), 2 * SUBLANES)
            for half in range(2)
        ]
        for m in range(ranks):
            cells = [b0[m, pl.ds(f, 1), :] * b1[m, qs, :] for f in first]
            cells = cells[0] if len(cells) == 1 else jnp.concatenate(cells, 0)
            high, low = split(cells)
            sa[at[0], m * own:(m + 1) * own] = high
            sa[at[1], m * own:(m + 1) * own] = low

    middle = slice(wide, wide + cols)
    flanks = (slice(0, wide), slice(wide + cols, wide + cols + wide))

    def fill_own(p, _):
        put(0, p * cols, (p + margin,), middle)
        return 0

    def fill_z(u, _):
        for n in range(2):
            put(1, n * rows * wide + u * 2 * wide, (2 * u + margin, 2 * u + 1 + margin), flanks[n])
        return 0

    def fill_x(u, _):
        for n in range(2):
            put(2, n * tall * cols + u * cols, (u + n * (rows + margin),), middle)
        return 0

    def fill_c(u, _):
        for n in range(4):
            first = 2 * u + (n // 2) * (rows + margin)
            put(3, n * tall * wide + u * 2 * wide, (first, first + 1), flanks[n % 2])
        return 0

    lax.fori_loop(0, rows // 2, fill_z, 0)
    lax.fori_loop(0, tall, fill_x, 0)
    lax.fori_loop(0, tall // 2, fill_c, 0)

    for copy in copies:
        copy.wait()

    step = step_ref[0]
    shrink = step * pen_ref[0]
    groups = [None, SIDES[0:2], SIDES[2:4], SIDES[4:8]]

    def doubled(cells):
        return jnp.concatenate([jnp.concatenate(split(cells), 1)] * 2, 0)

    def both(pair):
        return pair[:, :depth] + pair[:, depth:]

    for iteration in range(ITERS):
        phase = 2 * iteration
        for t in range(4):
            if t == 0:
                cells = x_ref[...]
            else:
                receive(phase, groups[t])
                cells = halo[t - 1][phase]
            right = doubled(cells.reshape(tile, depth))
            for m in range(ranks):
                at = slice(m * own, (m + 1) * own)
                part = jnp.dot(
                    sf[at, 2 * t * tile:(2 * t + 2) * tile], right, preferred_element_type=F32
                )
                acc[at] = part if t == 0 else acc[at] + part
        residual = -m_ref[...].reshape(own, depth)
        for m in range(ranks):
            at = slice(m * own, (m + 1) * own)
            mixed = jnp.concatenate(split(both(acc[at])), 1)
            blurred = both(jnp.dot(mixed, zf[m], preferred_element_type=F32))
            residual = residual + wv_ref[m].reshape(own, depth) * blurred
        for m in range(ranks):
            mixed = jnp.concatenate(split(wv_ref[m].reshape(own, depth) * residual), 1)
            back = both(jnp.dot(mixed, za[m], preferred_element_type=F32))
            v_ref[m * own:(m + 1) * own] = jnp.concatenate(split(back), 1)

        def spread(t):
            sums = jnp.dot(
                sa[2 * t * tile:(2 * t + 2) * tile], v_ref[...], preferred_element_type=F32
            )
            return both(sums[:tile] + sums[tile:])

        phase = phase + 1
        outgoing = (gz, gx_, gc)
        for t in (3, 1, 2):
            ref = outgoing[t - 1]
            ref[iteration] = spread(t).reshape(ref.shape[1:])
            send(phase, groups[t])
        if iteration == 0:
            lax.fori_loop(0, rows, fill_own, 0)
        acc[:own, :depth] = spread(0)
        grad = acc.at[:own, :depth]
        receive(phase, SIDES)
        total = grad[...].reshape(rows, cols, depth)
        inner = jnp.concatenate(
            [hz[phase, 0], hz[phase, 1]], 1
        ) if cols == 2 * wide else None
        total = total + inner
        lower = jnp.concatenate([hc[phase, 0], hc[phase, 1]], 1) + hx[phase, 0]
        upper = jnp.concatenate([hc[phase, 2], hc[phase, 3]], 1) + hx[phase, 1]
        lower = lower[:margin]
        upper = upper[:margin]
        gap = jnp.zeros((rows - margin, cols, depth), F32)
        total = total + jnp.concatenate([lower, gap], 0) + jnp.concatenate([gap, upper], 0)
        extrapolated = x_ref[...]
        current = extrapolated if iteration == 0 else cur_ref[...]
        moved = extrapolated - step * total
        updated = jnp.where(
            moved > shrink, moved - shrink, jnp.where(moved < -shrink, moved + shrink, 0.0)
        )
        if iteration + 1 == ITERS:
            delta_ref[...] = updated - current
            cur_ref[...] = current
            break
        x_ref[...] = updated + weight_of(iteration) * (updated - current)
        cur_ref[...] = updated
        send(phase + 1, order)

    for phase in range(2 * ITERS):
        for side in SIDES:
            @pl.when(there(side))
            def _():
                transfer(phase, side, source(phase, side)).wait_send()


def on_device(nx, ny, estimate, measured, weights, kernels, step_size, penalty):
    rows, cols, depth = estimate.shape
    ranks, _, taps = kernels.shape
    margin = taps // 2
    wide = -(-margin // SUBLANES) * SUBLANES
    tall = wide
    own = rows * cols
    assert cols == 2 * wide and rows == 2 * tall and ITERS >= 1
    phases = 2 * ITERS
    smem = pl.BlockSpec(memory_space=pltpu.SMEM)
    hbm = pl.BlockSpec(memory_space=pltpu.HBM)
    vmem = pl.BlockSpec(memory_space=pltpu.VMEM)

    def pieces(lead):
        return [
            pltpu.VMEM((lead, 2, rows, wide, depth), F32),
            pltpu.VMEM((lead, 2, tall, cols, depth), F32),
            pltpu.VMEM((lead, 4, tall, wide, depth), F32),
        ]

    out = jax.ShapeDtypeStruct(estimate.shape, F32)
    delta, current = pl.pallas_call(
        functools.partial(kernel, nx, ny, rows, cols, depth, taps, ranks),
        out_shape=(out, out),
        in_specs=[smem, smem, hbm, hbm, hbm, hbm],
        out_specs=(vmem, vmem),
        scratch_shapes=[
            pltpu.SMEM((kernels.shape[1], ranks, taps), F32),
            pltpu.VMEM(estimate.shape, F32),
            pltpu.VMEM(measured.shape, F32),
            pltpu.VMEM(weights.shape, F32),
            *pieces(phases),
            *pieces(ITERS),
            pltpu.VMEM((ranks, rows, 4 * own), F32),
            pltpu.VMEM((ranks, cols, 4 * own), F32),
            pltpu.VMEM((ranks, rows + 2 * tall, own), F32),
            pltpu.VMEM((ranks, cols + 2 * wide, own), F32),
            pltpu.VMEM((ranks * own, 8 * own), BF16),
            pltpu.VMEM((8 * own, ranks * own), BF16),
            pltpu.VMEM((ranks, 2 * depth, 2 * depth), BF16),
            pltpu.VMEM((ranks, 2 * depth, 2 * depth), BF16),
            pltpu.VMEM((ranks * own, 2 * depth), F32),
            pltpu.VMEM((ranks * own, 2 * depth), BF16),
            pltpu.SemaphoreType.DMA((4,)),
            pltpu.SemaphoreType.DMA((phases, len(SIDES))),
            pltpu.SemaphoreType.DMA((phases, len(SIDES))),
        ],
        compiler_params=pltpu.CompilerParams(
            collective_id=0, has_side_effects=True, vmem_limit_bytes=GRANT
        ),
        name="fista",
    )(
        step_size,
        penalty,
        *(
            pltpu.with_memory_space_constraint(array, pltpu.HBM)
            for array in (kernels.transpose(1, 0, 2), estimate, measured, weights)
        ),
    )
    updated = current + delta
    return updated, updated + weight_of(ITERS - 1) * delta


def solution(mesh):
    return jax.shard_map(
        functools.partial(on_device, mesh.shape["gx"], mesh.shape["gy"]),
        mesh=mesh,
        in_specs=(
            P("gx", "gy", None),
            P("gx", "gy", None),
            P(None, "gx", "gy", None),
            P(),
            P(),
            P(),
        ),
        out_specs=(P("gx", "gy", None), P("gx", "gy", None)),
        check_vma=False,
    )
```
